128 devices in a mesh: rows: 8 (over z, core), lag: 16 (over y, x).
Axes of the slice: x: 4, y: 4, z: 4, core: 2. Of those that a mesh axis runs over, the one named last changes fastest.
Arguments:
- excitation: bfloat16 [4, 4096, 128], P(None, 'rows'), may hold values from -6 to 6
- pending: float32 [16, 4096, 128], P('lag', 'rows'), may hold values from -6 to 6
- inverse: float32 [32, 128, 128], P('rows'), may hold values from -0.5 to 0.5
- interaction: bfloat16 [12288, 128, 128], P(('rows', 'lag')), may hold values from -0.02734375 to 0.02734375
- slot_row: int32 [12288], P(('rows', 'lag')), may hold values from 0 to 3
- slot_owner: int32 [12288], P(('rows', 'lag')), may hold values from 0 to 7
- slot_pos: int32 [12288], P(('rows', 'lag')), may hold values from 0 to 1
- needed: int32 [128, 8, 2], P(('rows', 'lag')), may hold values from 0 to 3
- block_count: int32 [8, 16], P('rows', 'lag'), may hold values from 6 to 96, as said below
Outputs:
- currents: bfloat16 [4, 4096, 128], P(None, 'rows')
- carried: float32 [16, 4096, 128], P('lag', 'rows')
The draws below stay inside these ranges and needn't reach their ends.
Inputs may be any that keep to these rules, and one draw needn't show every extreme that they name: `block_count`: every row owner and lag has at least 6 live slots, and some row owner and lag has all 96 live.
All inputs are finite; a program needn't handle non-finite values.
Results may differ from the reference program's by a relative error of at most 0.002.
Values may be sent and summed in bfloat16 or wider, within the bound.
No kernel may reach another device: no remote copies, remote signals or barrier semaphores. Data moves between devices by JAX's collectives and lax.ppermute only.
A program may use at most 64 MiB of HBM per device.

```python
import jax
import jax.numpy as jnp
from jax import lax

BLK = 128
EXC = 128
STEPS = 4
RB_DEV = 4
BPR = 24
K_DEV = 96
CAP = 2
ROW_BLOCKS = 32
UNKNOWNS = 4096
N_ROWS = 8
N_LAG = 16


def draw_block_count(key, part):
    first_key = jax.random.fold_in(key, 11)
    second_key = jax.random.fold_in(key, 23)
    uniform_count = jax.random.randint(first_key, (N_ROWS * N_LAG,), 0, K_DEV + 1)
    counted = jnp.maximum(K_DEV // 16, uniform_count * uniform_count // K_DEV)
    chosen = jax.random.randint(second_key, (), 0, N_ROWS * N_LAG)
    counted = jnp.where(jnp.arange(N_ROWS * N_LAG) == chosen, K_DEV, counted)
    return counted.reshape(N_ROWS, N_LAG).astype(jnp.int32)


def touch_ends(result, key, least, top_value):
    place = [jax.random.randint(jax.random.fold_in(key, axis), (), 0, length) for axis, length in enumerate(result.shape)]
    longest = result.shape.index(max(result.shape))
    beside = place[:longest] + [(place[longest] + 1) % result.shape[longest]] + place[longest + 1:]
    return result.at[tuple(place)].set(least).at[tuple(beside)].set(top_value)


def shard_levels(rng, extent, cuts, smallest, largest):
    gain, own = 1.0, jax.random.fold_in(rng, 6)
    for axis_at, blocks in cuts:
        draws = jnp.exp(jax.random.uniform(jax.random.fold_in(own, axis_at), (blocks,), jnp.float32, smallest / len(cuts), largest / len(cuts)))
        gain = gain * jnp.repeat(draws, extent[axis_at] // blocks).reshape([-1 if axis == axis_at else 1 for axis in range(len(extent))])
    return gain


def centred(own_key, shape, deviation, limit, pieces=(), kind=jnp.bfloat16):
    drawn = jax.random.normal(own_key, shape, jnp.float32) * deviation
    if len(pieces) > 0:
        drawn = shard_levels(own_key, shape, pieces, -0.22, 0.18) * drawn
    return jnp.clip(drawn, min=-limit, max=limit).astype(kind)


def setup_inputs(seed: int = 0) -> dict:
    seeds = jax.random.split(jax.random.key(seed), 10)
    return {
        "excitation": centred(seeds[0], (STEPS, UNKNOWNS, EXC), 1.0, 6.0, ((1, 8),)),
        "pending": centred(seeds[1], (N_LAG, UNKNOWNS, EXC), 1.0, 6.0, ((0, 16), (1, 8)), jnp.float32),
        "inverse": centred(seeds[2], (ROW_BLOCKS, BLK, BLK), BLK ** -0.5, 0.5, ((0, 8),), jnp.float32),
        "interaction": centred(seeds[3], (N_ROWS * N_LAG * K_DEV, BLK, BLK), (BLK * BPR * N_LAG) ** -0.5, 0.02734375, ((0, 128),)),
        "slot_row": touch_ends(jax.random.randint(seeds[4], (N_ROWS * N_LAG * K_DEV,), 0, RB_DEV), jax.random.fold_in(seeds[4], 1), 0, RB_DEV - 1).astype(jnp.int32),
        "slot_owner": touch_ends(jax.random.randint(seeds[5], (N_ROWS * N_LAG * K_DEV,), 0, N_ROWS), jax.random.fold_in(seeds[5], 1), 0, N_ROWS - 1).astype(jnp.int32),
        "slot_pos": touch_ends(jax.random.randint(seeds[6], (N_ROWS * N_LAG * K_DEV,), 0, CAP), jax.random.fold_in(seeds[6], 1), 0, CAP - 1).astype(jnp.int32),
        "needed": touch_ends(jax.random.randint(seeds[7], (N_ROWS * N_LAG, N_ROWS, CAP), 0, RB_DEV), jax.random.fold_in(seeds[7], 1), 0, RB_DEV - 1).astype(jnp.int32),
        "block_count": draw_block_count(jax.random.fold_in(seeds[9], 71), 0),
    }


def lag_terms(solved, interaction, slot_row, slot_owner, slot_pos, needed, block_count):
    blocks = solved.reshape(ROW_BLOCKS, BLK, EXC).astype(jnp.float32)
    inter_all = interaction.reshape(N_ROWS * N_LAG, K_DEV, BLK, BLK)
    rows_all = slot_row.reshape(N_ROWS * N_LAG, K_DEV)
    owner_all = slot_owner.reshape(N_ROWS * N_LAG, K_DEV)
    pos_all = slot_pos.reshape(N_ROWS * N_LAG, K_DEV)
    need_all = needed.reshape(N_ROWS * N_LAG, N_ROWS, CAP)
    count_all = block_count.reshape(N_ROWS * N_LAG)

    def lag_block(flat_index):
        need_table = need_all[flat_index]
        owners = owner_all[flat_index]
        local_block = need_table[owners, pos_all[flat_index]]
        column = (owners * RB_DEV + local_block).astype(jnp.int32)
        picked = blocks[column]
        products = jnp.einsum("kij,kje->kie", inter_all[flat_index].astype(jnp.float32), picked,
                              precision=lax.Precision.HIGHEST)
        live_slots = jnp.arange(K_DEV, dtype=jnp.int32) < count_all[flat_index]
        placing = ((rows_all[flat_index][None, :] == jnp.arange(RB_DEV, dtype=jnp.int32)[:, None])
                   & live_slots[None, :]).astype(jnp.float32)
        return jnp.einsum("bk,kie->bie", placing, products, precision=lax.Precision.HIGHEST)

    results = lax.map(lag_block, jnp.arange(N_ROWS * N_LAG, dtype=jnp.int32))
    results = results.reshape(N_ROWS, N_LAG, RB_DEV * BLK, EXC)
    return jnp.transpose(results, (1, 0, 2, 3)).reshape(N_LAG, UNKNOWNS, EXC)


def reference(excitation, pending, inverse, interaction, slot_row, slot_owner, slot_pos, needed, block_count):
    accumulated = pending
    outputs = []
    for step_index in range(STEPS):
        right_side = excitation[step_index].astype(jnp.float32) - accumulated[0]
        solved = jnp.einsum("bij,bje->bie", inverse, right_side.reshape(ROW_BLOCKS, BLK, EXC),
                            precision=lax.Precision.HIGHEST)
        solved = solved.reshape(UNKNOWNS, EXC).astype(jnp.bfloat16)
        outputs.append(solved)
        terms = lag_terms(solved, interaction, slot_row, slot_owner, slot_pos, needed, block_count)
        shifted = jnp.concatenate([accumulated[1:], jnp.zeros((1, UNKNOWNS, EXC), jnp.float32)], axis=0)
        accumulated = shifted + terms
    return jnp.stack(outputs), accumulated
```

```python
import jax
import jax.numpy as jnp
from jax import lax
from jax.experimental import pallas as pl
from jax.experimental.pallas import tpu as pltpu
from jax.sharding import PartitionSpec as P

UNROLL = 8


def accumulate(meta, blocks, pieces, base, gathered, sums):
    rows = base.shape[0]
    for place, piece in enumerate(pieces):
        gathered[pl.ds(place * rows, rows)] = piece[...]
    sums[pl.ds(0, rows)] = base[...]
    slots = blocks.shape[0]

    def group(at, carry):
        for offset in range(UNROLL):
            slot = at * UNROLL + offset
            word = meta[slot]
            column = word >> 3
            row = word & 7
            sums[row] += jnp.dot(
                blocks[slot], gathered[column], preferred_element_type=jnp.float32
            )
        return carry

    lax.fori_loop(0, (meta[slots] + UNROLL - 1) // UNROLL, group, 0)


def solve_rows(inverse, right_side):
    return jnp.dot(
        inverse, right_side, precision=lax.Precision.HIGHEST, preferred_element_type=jnp.float32
    ).astype(jnp.bfloat16)


def first_kernel(excitation, base, inverse, solved):
    for b in range(base.shape[0]):
        solved[b] = solve_rows(inverse[b], excitation[b].astype(jnp.float32) - base[b])


def step_kernel(meta, blocks, *refs):
    *pieces, base, excitation, inverse, total, solved, gathered, sums = refs
    accumulate(meta, blocks, pieces, base, gathered, sums)
    for b in range(base.shape[0]):
        total[b] = sums[b]
        solved[b] = solve_rows(inverse[b], excitation[b].astype(jnp.float32) - sums[b])


def last_kernel(meta, blocks, *refs):
    *pieces, base, total, gathered, sums = refs
    accumulate(meta, blocks, pieces, base, gathered, sums)
    total[...] = sums[pl.ds(0, base.shape[0])]


def scratch(pieces, base):
    rows, size, width = base.shape
    return [
        pltpu.VMEM((len(pieces) * rows, size, width), jnp.bfloat16),
        pltpu.VMEM((8, size, width), jnp.float32),
    ]


SMEM = pl.BlockSpec(memory_space=pltpu.SMEM)
VMEM = pl.BlockSpec(memory_space=pltpu.VMEM)


def first_solve(excitation, base, inverse):
    return pl.pallas_call(
        first_kernel,
        out_shape=jax.ShapeDtypeStruct(base.shape, jnp.bfloat16),
        in_specs=[VMEM] * 3,
        out_specs=VMEM,
    )(excitation, base, inverse)


def step(meta, blocks, pieces, base, excitation, inverse):
    return pl.pallas_call(
        step_kernel,
        out_shape=(
            jax.ShapeDtypeStruct(base.shape, jnp.float32),
            jax.ShapeDtypeStruct(base.shape, jnp.bfloat16),
        ),
        in_specs=[SMEM] + [VMEM] * (len(pieces) + 4),
        out_specs=(VMEM, VMEM),
        scratch_shapes=scratch(pieces, base),
    )(meta, blocks, *pieces, base, excitation, inverse)


def product(meta, blocks, pieces, base):
    return pl.pallas_call(
        last_kernel,
        out_shape=jax.ShapeDtypeStruct(base.shape, jnp.float32),
        in_specs=[SMEM] + [VMEM] * (len(pieces) + 2),
        out_specs=VMEM,
        scratch_shapes=scratch(pieces, base),
    )(meta, blocks, *pieces, base)


def over_rows(value, flip):
    count = lax.axis_size("rows")
    return lax.ppermute(value, "rows", [(r, r ^ flip) for r in range(count)])


def exchange(own):
    half = lax.axis_size("rows") // 2
    near = [own] + [over_rows(own, 2 * z) for z in range(1, half)]
    return near + [over_rows(piece, 1) for piece in near]


LAG_ROUNDS = (
    [(0, 1)],
    [(0, 3), (1, 2)],
    [(x, x + 4) for x in range(4)],
    [(x, x + 12) for x in range(4)] + [(x + 4, x + 8) for x in range(4)],
)


def spread(value):
    lag = lax.axis_index("lag")
    for pairs in LAG_ROUNDS:
        arrived = lax.ppermute(value, "lag", pairs)
        takes = jnp.zeros((), jnp.bool_)
        for _, target in pairs:
            takes = takes | (lag == target)
        value = jnp.where(takes, arrived, value)
    return value


def from_behind(value):
    count = lax.axis_size("lag")
    return lax.ppermute(value, "lag", [(g + 1, g) for g in range(count - 1)])


def slot_words(slot_row, slot_owner, slot_pos, needed, count):
    slots = slot_row.shape[0]
    table = needed.reshape(-1)
    entry = slot_owner * needed.shape[-1] + slot_pos
    local = jnp.sum(
        jnp.where(entry[:, None] == jnp.arange(table.shape[0], dtype=jnp.int32)[None, :], table[None, :], 0),
        axis=1,
    )
    apart = slot_owner ^ lax.axis_index("rows")
    column = ((apart & 1) * 4 + (apart >> 1)) * 4 + local
    row = jnp.where(jnp.arange(slots, dtype=jnp.int32) < count, slot_row, 4)
    return jnp.concatenate([column * 8 + row, jnp.full((32,), count, jnp.int32)])


def per_device(
    excitation, pending, inverse, interaction, slot_row, slot_owner, slot_pos, needed, block_count
):
    row_blocks, block_size, _ = inverse.shape
    steps, rows, width = excitation.shape
    excitation_blocks = excitation.reshape(steps, row_blocks, block_size, width)
    meta = slot_words(slot_row, slot_owner, slot_pos, needed[0], block_count[0, 0])
    total = pending[0].reshape(row_blocks, block_size, width)
    solved = first_solve(excitation_blocks[0], total, inverse)
    outputs = []
    for t in range(steps):
        base = from_behind(total)
        solved = spread(solved)
        outputs.append(solved)
        pieces = exchange(solved)
        if t + 1 < steps:
            total, solved = step(meta, interaction, pieces, base, excitation_blocks[t + 1], inverse)
        else:
            total = product(meta, interaction, pieces, base)
    return (jnp.stack(outputs).reshape(steps, rows, width), total.reshape(1, rows, width))


def solution(mesh):
    in_specs = (
        P(None, "rows", None),
        P("lag", "rows", None),
        P("rows", None, None),
        P(("rows", "lag"), None, None),
        P(("rows", "lag")),
        P(("rows", "lag")),
        P(("rows", "lag")),
        P(("rows", "lag"), None, None),
        P("rows", "lag"),
    )
    out_specs = (P(None, "rows", None), P("lag", "rows", None))
    return jax.shard_map(
        per_device, mesh=mesh, in_specs=in_specs, out_specs=out_specs, check_vma=False
    )
```

```python
import jax
import jax.numpy as jnp
from jax import lax
from jax.experimental import pallas as pl
from jax.experimental.pallas import tpu as pltpu
from jax.sharding import PartitionSpec as P


GROUP = 4
UNROLL = 4
PLACES = 112
ZERO_COLUMN = 32
COUNT_WORD = 144
PIECES = 8


def accumulate(meta, blocks, pieces, base, gathered, sums, arrivals):
    rows = base.shape[0]
    copies = [
        pltpu.make_async_copy(piece, gathered.at[pl.ds(place * rows, rows)], arrivals.at[place])
        for place, piece in enumerate(pieces)
    ]
    for copy in copies:
        copy.start()
    gathered[ZERO_COLUMN] = jnp.zeros(gathered.shape[1:], gathered.dtype)
    sums[...] = base[...]
    for copy in copies:
        copy.wait()

    def several(at, carry):
        for offset in range(UNROLL):
            group = at * UNROLL + offset
            words = [meta[group * GROUP + member] for member in range(GROUP)]
            left = jnp.concatenate([blocks[word >> 6] for word in words], axis=1)
            right = jnp.concatenate([gathered[word & 63] for word in words], axis=0)
            sums[meta[PLACES + group]] += jnp.dot(left, right, preferred_element_type=jnp.float32)
        return carry

    lax.fori_loop(0, (meta[COUNT_WORD] + UNROLL - 1) // UNROLL, several, 0)


def solve(inverse, excitation, field, solved):
    for b in range(inverse.shape[0]):
        solved[b] = jnp.dot(
            inverse[b],
            excitation[b].astype(jnp.float32) - field[b],
            precision=lax.Precision.HIGHEST,
            preferred_element_type=jnp.float32,
        ).astype(solved.dtype)


def first_kernel(lag, excitation, base, inverse, solved):
    @pl.when(lag[0] == 0)
    def _():
        solve(inverse, excitation, base, solved)

    @pl.when(lag[0] != 0)
    def _():
        solved[...] = jnp.zeros(solved.shape, solved.dtype)


def chain_kernel(lag, meta, blocks, *refs):
    pieces, (base, excitation, inverse, solved, gathered, sums, arrivals) = refs[:PIECES], refs[PIECES:]

    @pl.when(lag[0] == 0)
    def _():
        accumulate(meta, blocks, pieces, base, gathered, sums, arrivals)
        solve(inverse, excitation, sums, solved)

    @pl.when(lag[0] != 0)
    def _():
        solved[...] = jnp.zeros(solved.shape, solved.dtype)


def others_kernel(lag, meta, blocks, *refs):
    pieces, (base, total, gathered, arrivals) = refs[:PIECES], refs[PIECES:]

    @pl.when(lag[0] != 0)
    def _():
        accumulate(meta, blocks, pieces, base, gathered, total, arrivals)

    @pl.when(lag[0] == 0)
    def _():
        total[...] = jnp.zeros(total.shape, total.dtype)


def last_kernel(meta, blocks, *refs):
    pieces, solved, (base, total, kept, gathered, arrivals, placed) = refs[:PIECES], refs[PIECES:-6], refs[-6:]
    copies = [
        pltpu.make_async_copy(each, kept.at[t], placed.at[t]) for t, each in enumerate(solved)
    ]
    for copy in copies:
        copy.start()
    accumulate(meta, blocks, pieces, base, gathered, total, arrivals)
    for copy in copies:
        copy.wait()


PARAMS = pltpu.CompilerParams(vmem_limit_bytes=24 * 1024 * 1024)
SMEM = pl.BlockSpec(memory_space=pltpu.SMEM)
VMEM = pl.BlockSpec(memory_space=pltpu.VMEM)
ANY = pl.BlockSpec(memory_space=pl.ANY)


def held(arrays):
    return [pltpu.with_memory_space_constraint(array, pltpu.VMEM) for array in arrays]


def gathering(base):
    return [
        pltpu.VMEM((ZERO_COLUMN + 1,) + base.shape[1:], jnp.bfloat16),
        pltpu.SemaphoreType.DMA((PIECES,)),
    ]


def first_solve(lag, excitation, base, inverse):
    return pl.pallas_call(
        first_kernel,
        out_shape=jax.ShapeDtypeStruct(base.shape, jnp.bfloat16),
        in_specs=[SMEM, VMEM, VMEM, VMEM],
        compiler_params=PARAMS,
        out_specs=VMEM,
    )(lag, excitation, base, inverse)


def chain_step(lag, meta, blocks, pieces, base, excitation, inverse):
    gathered, arrivals = gathering(base)
    return pl.pallas_call(
        chain_kernel,
        out_shape=jax.ShapeDtypeStruct(base.shape, jnp.bfloat16),
        in_specs=[SMEM, SMEM, VMEM] + [VMEM] * PIECES + [VMEM] * 3,
        compiler_params=PARAMS,
        out_specs=VMEM,
        scratch_shapes=[gathered, pltpu.VMEM(base.shape, jnp.float32), arrivals],
    )(lag, meta, blocks, *held(pieces), base, excitation, inverse)


def others_step(lag, meta, blocks, pieces, base):
    return pl.pallas_call(
        others_kernel,
        out_shape=jax.ShapeDtypeStruct(base.shape, jnp.float32),
        in_specs=[SMEM, SMEM, VMEM] + [VMEM] * PIECES + [VMEM],
        compiler_params=PARAMS,
        out_specs=VMEM,
        scratch_shapes=gathering(base),
    )(lag, meta, blocks, *held(pieces), base)


def last_step(meta, blocks, pieces, solved, base):
    return pl.pallas_call(
        last_kernel,
        out_shape=(
            jax.ShapeDtypeStruct(base.shape, jnp.float32),
            jax.ShapeDtypeStruct((len(solved),) + base.shape, jnp.bfloat16),
        ),
        in_specs=[SMEM, VMEM] + [VMEM] * PIECES + [ANY] * len(solved) + [VMEM],
        compiler_params=PARAMS,
        out_specs=(VMEM, ANY),
        scratch_shapes=gathering(base) + [pltpu.SemaphoreType.DMA((len(solved),))],
    )(meta, blocks, *held(pieces), *solved, base)


def over_rows(value, flip):
    count = lax.axis_size("rows")
    return lax.ppermute(value, "rows", [(r, r ^ flip) for r in range(count)])


def exchange(own):
    half = lax.axis_size("rows") // 2
    near = [own]
    for z in range(1, half):
        near.append(over_rows(own, 2 * z))
    pieces = list(near)
    for z in range(half):
        pieces.append(over_rows(near[z], 1))
    return pieces


LAG_ROUNDS = (
    [(0, 1)],
    [(0, 3), (1, 2)],
    [(x, x + 4) for x in range(4)],
    [(x, x + 12) for x in range(4)] + [(x + 4, x + 8) for x in range(4)],
)


def spread(value):
    lag = lax.axis_index("lag")
    for pairs in LAG_ROUNDS:
        arrived = lax.ppermute(value, "lag", pairs)
        takes = jnp.zeros((), jnp.bool_)
        for _, target in pairs:
            takes = takes | (lag == target)
        value = jnp.where(takes, arrived, value)
    return value


def from_behind(value):
    count = lax.axis_size("lag")
    return lax.ppermute(value, "lag", [(g + 1, g) for g in range(count - 1)])


def slot_words(slot_row, slot_owner, slot_pos, needed, count, row_blocks):
    slots = slot_row.shape[0]
    at = jnp.arange(slots, dtype=jnp.int32)
    live = at < count
    table = needed.reshape(-1)
    entry = slot_owner * needed.shape[-1] + slot_pos
    entries = jnp.arange(table.shape[0], dtype=jnp.int32)
    local = jnp.sum(jnp.where(entry[:, None] == entries[None, :], table[None, :], 0), axis=1)
    apart = slot_owner ^ lax.axis_index("rows")
    column = ((apart & 1) * 4 + (apart >> 1)) * row_blocks + local
    word = at * 64 + column
    earlier = (slot_row[None, :] == slot_row[:, None]) & (at[None, :] < at[:, None])
    rank = jnp.sum(earlier.astype(jnp.int32), axis=1)
    row_at = jnp.arange(row_blocks, dtype=jnp.int32)
    in_row = (slot_row[None, :] == row_at[:, None]) & live[None, :]
    groups = (jnp.sum(in_row.astype(jnp.int32), axis=1) + GROUP - 1) // GROUP
    first = jnp.sum(jnp.where(row_at[None, :] < row_at[:, None], groups[None, :], 0), axis=1)
    start = jnp.sum(jnp.where(slot_row[:, None] == row_at[None, :], first[None, :], 0), axis=1)
    place = jnp.where(live, start * GROUP + rank, -1)
    taken = place[None, :] == jnp.arange(PLACES, dtype=jnp.int32)[:, None]
    words = ZERO_COLUMN + jnp.sum(jnp.where(taken, word[None, :] - ZERO_COLUMN, 0), axis=1)
    group_at = jnp.arange(COUNT_WORD - PLACES, dtype=jnp.int32)
    group_row = jnp.sum((group_at[:, None] >= first[None, :]).astype(jnp.int32), axis=1) - 1
    return jnp.concatenate([words, group_row, jnp.sum(groups)[None]])


def per_device(
    excitation, pending, inverse, interaction, slot_row, slot_owner, slot_pos, needed, block_count
):
    row_blocks, block_size, _ = inverse.shape
    steps, rows, width = excitation.shape
    excitation_blocks = excitation.reshape(steps, row_blocks, block_size, width)
    lag = jnp.full((1,), lax.axis_index("lag"), jnp.int32)
    total = pending[0].reshape(row_blocks, block_size, width)
    solved = first_solve(lag, excitation_blocks[0], total, inverse)
    slot_row, solved = lax.optimization_barrier((slot_row, solved))
    meta = slot_words(slot_row, slot_owner, slot_pos, needed[0], block_count[0, 0], row_blocks)
    outputs = []
    (interaction,) = held((interaction,))
    for t in range(steps):
        solved = spread(solved)
        outputs.append(solved)
        if t > 0:
            total = others_step(lag, meta, interaction, pieces, base)
        base = from_behind(total)
        pieces = exchange(solved)
        if t + 1 < steps:
            solved = chain_step(lag, meta, interaction, pieces, base, excitation_blocks[t + 1], inverse)
        else:
            total, kept = last_step(meta, interaction, pieces, outputs, base)
    return (kept.reshape(steps, rows, width), total.reshape(1, rows, width))


def solution(mesh):
    in_specs = (
        P(None, "rows", None),
        P("lag", "rows", None),
        P("rows", None, None),
        P(("rows", "lag"), None, None),
        P(("rows", "lag")),
        P(("rows", "lag")),
        P(("rows", "lag")),
        P(("rows", "lag"), None, None),
        P("rows", "lag"),
    )
    out_specs = (P(None, "rows", None), P("lag", "rows", None))
    return jax.shard_map(
        per_device, mesh=mesh, in_specs=in_specs, out_specs=out_specs, check_vma=False
    )
```

```python
import functools

import jax
import jax.numpy as jnp
from jax import lax
from jax.experimental import pallas as pl
from jax.experimental.pallas import tpu as pltpu
from jax.sharding import PartitionSpec as P


GROUP = 4
UNROLL = 9
GROUPS = 27
PLACES = GROUP * GROUPS
ZERO_COLUMN = 32
COUNT_WORD = PLACES + GROUPS
PIECES = 8


def accumulate(meta, blocks, pieces, base, gathered, sums, arrivals):
    rows = base.shape[0]
    copies = [
        pltpu.make_async_copy(piece, gathered.at[pl.ds(place * rows, rows)], arrivals.at[place])
        for place, piece in enumerate(pieces)
    ]
    for copy in copies:
        copy.start()
    gathered[ZERO_COLUMN] = jnp.zeros(gathered.shape[1:], gathered.dtype)
    sums[...] = base[...]
    for copy in copies:
        copy.wait()

    def several(at, carry):
        for offset in range(UNROLL):
            group = at * UNROLL + offset
            words = [meta[group * GROUP + member] for member in range(GROUP)]
            left = jnp.concatenate([blocks[word >> 6] for word in words], axis=1)
            right = jnp.concatenate([gathered[word & 63] for word in words], axis=0)
            sums[meta[PLACES + group]] += jnp.dot(left, right, preferred_element_type=jnp.float32)
        return carry

    lax.fori_loop(0, (meta[COUNT_WORD] + UNROLL - 1) // UNROLL, several, 0)


def parts(value):
    high = value.astype(jnp.bfloat16)
    return high, (value - high.astype(jnp.float32)).astype(jnp.bfloat16)


def solve(inverse, excitation, field, solved):
    for b in range(inverse.shape[0]):
        high, low = parts(inverse[b])
        right_high, right_low = parts(excitation[b].astype(jnp.float32) - field[b])
        solved[b] = jnp.dot(
            jnp.concatenate([high, high, low], axis=1),
            jnp.concatenate([right_high, right_low, right_high], axis=0),
            preferred_element_type=jnp.float32,
        ).astype(solved.dtype)


def words_kernel(place_of, tables, *refs):
    kept, held_refs, (words, tally, arrivals) = refs[:3], refs[4:7], (refs[3],) + refs[7:]
    moves = [
        pltpu.make_async_copy(source, target, arrivals.at[at])
        for at, (source, target) in enumerate(zip(kept, held_refs))
    ]
    for copy in moves:
        copy.start()
    slots = (tables.shape[0] - 2 * PIECES - 1) // 3
    live = tables[3 * slots + 2 * PIECES]
    rows = tally.shape[0]
    for b in range(rows):
        tally[b] = 0

    def clear(at, carry):
        words[at] = jnp.where(at < PLACES, ZERO_COLUMN, 0)
        return carry

    lax.fori_loop(0, COUNT_WORD + 1, clear, 0, unroll=8)

    def count_row(slot, carry):
        tally[tables[slot]] += 1
        return carry

    lax.fori_loop(0, live, count_row, 0)
    first = 0
    for b in range(rows):
        groups = (tally[b] + GROUP - 1) // GROUP

        def name_row(group, carry, b=b):
            words[PLACES + group] = b
            return carry

        tally[b] = first * GROUP
        lax.fori_loop(first, first + groups, name_row, 0)
        first = first + groups
    words[COUNT_WORD] = first

    def put(slot, carry):
        row = tables[slot]
        place = tally[row]
        tally[row] = place + 1
        owner = tables[slots + slot]
        apart = owner ^ place_of[1]
        piece = (apart & 1) * (PIECES // 2) + (apart >> 1)
        local = tables[3 * slots + tables[2 * slots + slot] * PIECES + owner]
        words[place] = slot * 64 + piece * rows + local
        return carry

    lax.fori_loop(0, live, put, 0)
    for copy in moves:
        copy.wait()


def first_kernel(place_of, excitation, base, inverse, solved, right, field, factors, arrivals):
    @pl.when(place_of[0] == 0)
    def _():
        copies = [
            pltpu.make_async_copy(excitation.at[0], right, arrivals.at[0]),
            pltpu.make_async_copy(base, field, arrivals.at[1]),
            pltpu.make_async_copy(inverse, factors, arrivals.at[2]),
        ]
        for copy in copies:
            copy.start()
        for copy in copies:
            copy.wait()
        solve(factors, right, field, solved)

    @pl.when(place_of[0] != 0)
    def _():
        solved[...] = jnp.zeros(solved.shape, solved.dtype)


def chain_kernel(t, place_of, meta, blocks, *refs):
    pieces, (base, excitation, inverse, solved, gathered, sums, arrivals) = refs[:PIECES], refs[PIECES:]

    @pl.when(place_of[0] == 0)
    def _():
        accumulate(meta, blocks, pieces, base, gathered, sums, arrivals)
        solve(inverse, excitation.at[t], sums, solved)

    @pl.when(place_of[0] != 0)
    def _():
        solved[...] = jnp.zeros(solved.shape, solved.dtype)


def others_kernel(place_of, meta, blocks, *refs):
    pieces, (base, total, gathered, arrivals) = refs[:PIECES], refs[PIECES:]

    @pl.when(place_of[0] != 0)
    def _():
        accumulate(meta, blocks, pieces, base, gathered, total, arrivals)

    @pl.when(place_of[0] == 0)
    def _():
        total[...] = jnp.zeros(total.shape, total.dtype)


def last_kernel(meta, blocks, *refs):
    pieces, solved, (base, total, kept, gathered, arrivals, placed) = refs[:PIECES], refs[PIECES:-6], refs[-6:]
    copies = [
        pltpu.make_async_copy(each, kept.at[t], placed.at[t]) for t, each in enumerate(solved)
    ]
    for copy in copies:
        copy.start()
    accumulate(meta, blocks, pieces, base, gathered, total, arrivals)
    for copy in copies:
        copy.wait()


PARAMS = pltpu.CompilerParams(vmem_limit_bytes=24 * 1024 * 1024)
SMEM = pl.BlockSpec(memory_space=pltpu.SMEM)
VMEM = pl.BlockSpec(memory_space=pltpu.VMEM)
ANY = pl.BlockSpec(memory_space=pl.ANY)
HBM = pl.BlockSpec(memory_space=pltpu.HBM)


def held(arrays):
    return [pltpu.with_memory_space_constraint(array, pltpu.VMEM) for array in arrays]


def gathering(base):
    return [
        pltpu.VMEM((ZERO_COLUMN + 1,) + base.shape[1:], jnp.bfloat16),
        pltpu.SemaphoreType.DMA((PIECES,)),
    ]


def prepare(place_of, tables, kept, row_blocks):
    shapes = [jax.ShapeDtypeStruct(each.shape, each.dtype) for each in kept]
    words, *held_arrays = pl.pallas_call(
        words_kernel,
        out_shape=[jax.ShapeDtypeStruct((COUNT_WORD + 1,), jnp.int32)] + shapes,
        in_specs=[SMEM, SMEM] + [HBM] * len(kept),
        compiler_params=pltpu.CompilerParams(vmem_limit_bytes=48 * 1024 * 1024),
        out_specs=[SMEM] + [VMEM] * len(kept),
        scratch_shapes=[
            pltpu.SMEM((row_blocks,), jnp.int32),
            pltpu.SemaphoreType.DMA((len(kept),)),
        ],
    )(place_of, tables, *kept)
    return words, held(held_arrays)


def first_solve(place_of, excitation, base, inverse):
    return pl.pallas_call(
        first_kernel,
        out_shape=jax.ShapeDtypeStruct(base.shape, jnp.bfloat16),
        in_specs=[SMEM, HBM, HBM, HBM],
        out_specs=VMEM,
        scratch_shapes=[
            pltpu.VMEM(base.shape, jnp.bfloat16),
            pltpu.VMEM(base.shape, jnp.float32),
            pltpu.VMEM(inverse.shape, jnp.float32),
            pltpu.SemaphoreType.DMA((3,)),
        ],
    )(place_of, excitation, base, inverse)


def chain_step(t, place_of, meta, blocks, pieces, base, excitation, inverse):
    gathered, arrivals = gathering(base)
    return pl.pallas_call(
        functools.partial(chain_kernel, t),
        out_shape=jax.ShapeDtypeStruct(base.shape, jnp.bfloat16),
        in_specs=[SMEM, SMEM, VMEM] + [VMEM] * PIECES + [VMEM] * 3,
        compiler_params=PARAMS,
        out_specs=VMEM,
        scratch_shapes=[gathered, pltpu.VMEM(base.shape, jnp.float32), arrivals],
    )(place_of, meta, blocks, *held(pieces), base, excitation, inverse)


def others_step(place_of, meta, blocks, pieces, base):
    return pl.pallas_call(
        others_kernel,
        out_shape=jax.ShapeDtypeStruct(base.shape, jnp.float32),
        in_specs=[SMEM, SMEM, VMEM] + [VMEM] * PIECES + [VMEM],
        compiler_params=PARAMS,
        out_specs=VMEM,
        scratch_shapes=gathering(base),
    )(place_of, meta, blocks, *held(pieces), base)


def last_step(meta, blocks, pieces, solved, base):
    return pl.pallas_call(
        last_kernel,
        out_shape=(
            jax.ShapeDtypeStruct(base.shape, jnp.float32),
            jax.ShapeDtypeStruct((len(solved),) + base.shape, jnp.bfloat16),
        ),
        in_specs=[SMEM, VMEM] + [VMEM] * PIECES + [ANY] * len(solved) + [VMEM],
        compiler_params=PARAMS,
        out_specs=(VMEM, ANY),
        scratch_shapes=gathering(base) + [pltpu.SemaphoreType.DMA((len(solved),))],
    )(meta, blocks, *held(pieces), *solved, base)


def over_rows(value, flip):
    count = lax.axis_size("rows")
    return lax.ppermute(value, "rows", [(r, r ^ flip) for r in range(count)])


def exchange(own):
    half = lax.axis_size("rows") // 2
    near = [own]
    for z in range(1, half):
        near.append(over_rows(own, 2 * z))
    pieces = list(near)
    for z in range(half):
        pieces.append(over_rows(near[z], 1))
    return pieces


LAG_ROUNDS = (
    [(0, 1)],
    [(0, 3), (1, 2)],
    [(x, x + 4) for x in range(4)],
    [(x, x + 12) for x in range(4)] + [(x + 4, x + 8) for x in range(4)],
)


def spread(value):
    lag = lax.axis_index("lag")
    for pairs in LAG_ROUNDS:
        arrived = lax.ppermute(value, "lag", pairs)
        takes = jnp.zeros((), jnp.bool_)
        for _, target in pairs:
            takes = takes | (lag == target)
        value = jnp.where(takes, arrived, value)
    return value


def from_behind(value):
    count = lax.axis_size("lag")
    return lax.ppermute(value, "lag", [(g + 1, g) for g in range(count - 1)])


def per_device(
    excitation, pending, inverse, interaction, slot_row, slot_owner, slot_pos, needed, block_count
):
    row_blocks, block_size, _ = inverse.shape
    steps, rows, width = excitation.shape
    excitation_blocks = excitation.reshape(steps, row_blocks, block_size, width)
    place_of = jnp.stack([lax.axis_index("lag"), lax.axis_index("rows")]).astype(jnp.int32)
    total = pending[0].reshape(row_blocks, block_size, width)
    solved = first_solve(place_of, excitation_blocks, total, inverse)
    tables = (slot_row, slot_owner, slot_pos, needed.transpose(0, 2, 1), block_count)
    tables = jnp.concatenate([table.reshape(-1) for table in tables])
    meta, (blocks, excitation_held, inverse_held) = prepare(
        place_of, tables, (interaction, excitation_blocks, inverse), row_blocks
    )
    outputs = []
    for t in range(steps):
        solved = spread(solved)
        outputs.append(solved)
        if t > 0:
            total = others_step(place_of, meta, blocks, pieces, base)
        base = from_behind(total)
        pieces = exchange(solved)
        if t + 1 < steps:
            solved = chain_step(
                t + 1, place_of, meta, blocks, pieces, base, excitation_held, inverse_held
            )
        else:
            total, kept = last_step(meta, blocks, pieces, outputs, base)
    return (kept.reshape(steps, rows, width), total.reshape(1, rows, width))


def solution(mesh):
    in_specs = (
        P(None, "rows", None),
        P("lag", "rows", None),
        P("rows", None, None),
        P(("rows", "lag"), None, None),
        P(("rows", "lag")),
        P(("rows", "lag")),
        P(("rows", "lag")),
        P(("rows", "lag"), None, None),
        P("rows", "lag"),
    )
    out_specs = (P(None, "rows", None), P("lag", "rows", None))
    return jax.shard_map(
        per_device, mesh=mesh, in_specs=in_specs, out_specs=out_specs, check_vma=False
    )
```

```python
import functools

import jax
import jax.numpy as jnp
from jax import lax
from jax.experimental import pallas as pl
from jax.experimental.pallas import tpu as pltpu
from jax.sharding import PartitionSpec as P


GROUP = 4
UNROLL = 9
GROUPS = 27
PLACES = GROUP * GROUPS
ZERO_COLUMN = 32
COUNT_WORD = PLACES + GROUPS
PIECES = 8


def accumulate(meta, blocks, pieces, base, gathered, sums):
    rows = base.shape[0]
    for place, piece in enumerate(pieces):
        gathered[pl.ds(place * rows, rows)] = piece[...]
    gathered[ZERO_COLUMN] = jnp.zeros(gathered.shape[1:], gathered.dtype)
    sums[...] = base[...]

    def several(at, carry):
        for offset in range(UNROLL):
            group = at * UNROLL + offset
            words = [meta[group * GROUP + member] for member in range(GROUP)]
            left = jnp.concatenate([blocks[word >> 6] for word in words], axis=1)
            right = jnp.concatenate([gathered[word & 63] for word in words], axis=0)
            sums[meta[PLACES + group]] += jnp.dot(left, right, preferred_element_type=jnp.float32)
        return carry

    lax.fori_loop(0, (meta[COUNT_WORD] + UNROLL - 1) // UNROLL, several, 0)


def parts(value):
    high = value.astype(jnp.bfloat16)
    return high, (value - high.astype(jnp.float32)).astype(jnp.bfloat16)


def solve(inverse, excitation, field, solved):
    for b in range(inverse.shape[0]):
        high, low = parts(inverse[b])
        right_high, right_low = parts(excitation[b].astype(jnp.float32) - field[b])
        solved[b] = jnp.dot(
            jnp.concatenate([high, high, low], axis=1),
            jnp.concatenate([right_high, right_low, right_high], axis=0),
            preferred_element_type=jnp.float32,
        ).astype(solved.dtype)


def words_kernel(tables, *refs):
    kept, held_refs, (words, tally, arrivals) = refs[:3], refs[4:7], (refs[3],) + refs[7:]
    moves = [
        pltpu.make_async_copy(source, target, arrivals.at[at])
        for at, (source, target) in enumerate(zip(kept, held_refs))
    ]
    for copy in moves:
        copy.start()
    slots = (tables.shape[0] - 2 * PIECES - 2) // 3
    live = tables[3 * slots + 2 * PIECES]
    rows = tally.shape[0]
    for b in range(rows):
        tally[b] = 0

    def clear(at, carry):
        words[at] = jnp.where(at < PLACES, ZERO_COLUMN, 0)
        return carry

    lax.fori_loop(0, COUNT_WORD + 1, clear, 0, unroll=8)

    def count_row(slot, carry):
        tally[tables[slot]] += 1
        return carry

    lax.fori_loop(0, live, count_row, 0)
    first = 0
    for b in range(rows):
        groups = (tally[b] + GROUP - 1) // GROUP

        def name_row(group, carry, b=b):
            words[PLACES + group] = b
            return carry

        tally[b] = first * GROUP
        lax.fori_loop(first, first + groups, name_row, 0)
        first = first + groups
    words[COUNT_WORD] = first

    def put(slot, carry):
        row = tables[slot]
        place = tally[row]
        tally[row] = place + 1
        owner = tables[slots + slot]
        apart = owner ^ tables[tables.shape[0] - 1]
        piece = (apart & 1) * (PIECES // 2) + (apart >> 1)
        local = tables[3 * slots + tables[2 * slots + slot] * PIECES + owner]
        words[place] = slot * 64 + piece * rows + local
        return carry

    lax.fori_loop(0, live, put, 0)
    for copy in moves:
        copy.wait()


def first_kernel(lag, excitation, base, inverse, solved, right, field, factors, arrivals):
    @pl.when(lag[0] == 0)
    def _():
        copies = [
            pltpu.make_async_copy(excitation.at[0], right, arrivals.at[0]),
            pltpu.make_async_copy(base, field, arrivals.at[1]),
            pltpu.make_async_copy(inverse, factors, arrivals.at[2]),
        ]
        for copy in copies:
            copy.start()
        for copy in copies:
            copy.wait()
        solve(factors, right, field, solved)

    @pl.when(lag[0] != 0)
    def _():
        solved[...] = jnp.zeros(solved.shape, solved.dtype)


def chain_kernel(t, lag, meta, blocks, *refs):
    pieces, (base, excitation, inverse, solved, gathered, sums) = refs[:PIECES], refs[PIECES:]

    @pl.when(lag[0] == 0)
    def _():
        accumulate(meta, blocks, pieces, base, gathered, sums)
        solve(inverse, excitation.at[t], sums, solved)

    @pl.when(lag[0] != 0)
    def _():
        solved[...] = jnp.zeros(solved.shape, solved.dtype)


def others_kernel(lag, meta, blocks, *refs):
    pieces, (base, total, gathered) = refs[:PIECES], refs[PIECES:]

    @pl.when(lag[0] != 0)
    def _():
        accumulate(meta, blocks, pieces, base, gathered, total)

    @pl.when(lag[0] == 0)
    def _():
        total[...] = jnp.zeros(total.shape, total.dtype)


def last_kernel(meta, blocks, *refs):
    pieces, solved, (base, total, kept, gathered, placed) = refs[:PIECES], refs[PIECES:-5], refs[-5:]
    copies = [
        pltpu.make_async_copy(each, kept.at[t], placed.at[t]) for t, each in enumerate(solved)
    ]
    for copy in copies:
        copy.start()
    accumulate(meta, blocks, pieces, base, gathered, total)
    for copy in copies:
        copy.wait()


PARAMS = pltpu.CompilerParams(vmem_limit_bytes=24 * 1024 * 1024)
SMEM = pl.BlockSpec(memory_space=pltpu.SMEM)
VMEM = pl.BlockSpec(memory_space=pltpu.VMEM)
ANY = pl.BlockSpec(memory_space=pl.ANY)
HBM = pl.BlockSpec(memory_space=pltpu.HBM)


def held(arrays):
    return [pltpu.with_memory_space_constraint(array, pltpu.VMEM) for array in arrays]


def gathering(base):
    return pltpu.VMEM((ZERO_COLUMN + 1,) + base.shape[1:], jnp.bfloat16)


def prepare(tables, kept, row_blocks):
    shapes = [jax.ShapeDtypeStruct(each.shape, each.dtype) for each in kept]
    words, *held_arrays = pl.pallas_call(
        words_kernel,
        out_shape=[jax.ShapeDtypeStruct((COUNT_WORD + 1,), jnp.int32)] + shapes,
        in_specs=[SMEM] + [HBM] * len(kept),
        compiler_params=pltpu.CompilerParams(vmem_limit_bytes=48 * 1024 * 1024),
        out_specs=[SMEM] + [VMEM] * len(kept),
        scratch_shapes=[
            pltpu.SMEM((row_blocks,), jnp.int32),
            pltpu.SemaphoreType.DMA((len(kept),)),
        ],
    )(tables, *kept)
    return words, held(held_arrays)


def first_solve(lag, excitation, base, inverse):
    return pl.pallas_call(
        first_kernel,
        out_shape=jax.ShapeDtypeStruct(base.shape, jnp.bfloat16),
        in_specs=[SMEM, HBM, HBM, HBM],
        out_specs=VMEM,
        scratch_shapes=[
            pltpu.VMEM(base.shape, jnp.bfloat16),
            pltpu.VMEM(base.shape, jnp.float32),
            pltpu.VMEM(inverse.shape, jnp.float32),
            pltpu.SemaphoreType.DMA((3,)),
        ],
    )(lag, excitation, base, inverse)


def chain_step(t, lag, meta, blocks, pieces, base, excitation, inverse):
    return pl.pallas_call(
        functools.partial(chain_kernel, t),
        out_shape=jax.ShapeDtypeStruct(base.shape, jnp.bfloat16),
        in_specs=[SMEM, SMEM, VMEM] + [VMEM] * PIECES + [VMEM] * 3,
        compiler_params=PARAMS,
        out_specs=VMEM,
        scratch_shapes=[gathering(base), pltpu.VMEM(base.shape, jnp.float32)],
    )(lag, meta, blocks, *held(pieces), base, excitation, inverse)


def others_step(lag, meta, blocks, pieces, base):
    return pl.pallas_call(
        others_kernel,
        out_shape=jax.ShapeDtypeStruct(base.shape, jnp.float32),
        in_specs=[SMEM, SMEM, VMEM] + [VMEM] * PIECES + [VMEM],
        compiler_params=PARAMS,
        out_specs=VMEM,
        scratch_shapes=[gathering(base)],
    )(lag, meta, blocks, *held(pieces), base)


def last_step(meta, blocks, pieces, solved, base):
    return pl.pallas_call(
        last_kernel,
        out_shape=(
            jax.ShapeDtypeStruct(base.shape, jnp.float32),
            jax.ShapeDtypeStruct((len(solved),) + base.shape, jnp.bfloat16),
        ),
        in_specs=[SMEM, VMEM] + [VMEM] * PIECES + [ANY] * len(solved) + [VMEM],
        compiler_params=PARAMS,
        out_specs=(VMEM, ANY),
        scratch_shapes=[gathering(base), pltpu.SemaphoreType.DMA((len(solved),))],
    )(meta, blocks, *held(pieces), *solved, base)


def over_rows(value, flip):
    count = lax.axis_size("rows")
    return lax.ppermute(value, "rows", [(r, r ^ flip) for r in range(count)])


def exchange(own):
    half = lax.axis_size("rows") // 2
    near = [own]
    for z in range(1, half):
        near.append(over_rows(own, 2 * z))
    pieces = list(near)
    for z in range(half):
        pieces.append(over_rows(near[z], 1))
    return pieces


LAG_ROUNDS = (
    [(0, 1)],
    [(0, 3), (1, 2)],
    [(x, x + 4) for x in range(4)],
    [(x, x + 12) for x in range(4)] + [(x + 4, x + 8) for x in range(4)],
)


def spread(value):
    lag = lax.axis_index("lag")
    for pairs in LAG_ROUNDS:
        arrived = lax.ppermute(value, "lag", pairs)
        takes = jnp.zeros((), jnp.bool_)
        for _, target in pairs:
            takes = takes | (lag == target)
        value = jnp.where(takes, arrived, value)
    return value


def from_behind(value):
    count = lax.axis_size("lag")
    return lax.ppermute(value, "lag", [(g + 1, g) for g in range(count - 1)])


def per_device(
    excitation, pending, inverse, interaction, slot_row, slot_owner, slot_pos, needed, block_count
):
    row_blocks, block_size, _ = inverse.shape
    steps, rows, width = excitation.shape
    excitation_blocks = excitation.reshape(steps, row_blocks, block_size, width)
    lag = jnp.full((1,), lax.axis_index("lag"), jnp.int32)
    row_owner = jnp.full((1,), lax.axis_index("rows"), jnp.int32)
    total = pending[0].reshape(row_blocks, block_size, width)
    solved = first_solve(lag, excitation_blocks, total, inverse)
    tables = (slot_row, slot_owner, slot_pos, needed.transpose(0, 2, 1), block_count, row_owner)
    tables = jnp.concatenate([table.reshape(-1) for table in tables])
    meta, (blocks, excitation_held, inverse_held) = prepare(
        tables, (interaction, excitation_blocks, inverse), row_blocks
    )
    outputs = []
    for t in range(steps):
        solved = spread(solved)
        outputs.append(solved)
        if t > 0:
            total = others_step(lag, meta, blocks, pieces, base)
        base = from_behind(total)
        pieces = exchange(solved)
        if t + 1 < steps:
            solved = chain_step(
                t + 1, lag, meta, blocks, pieces, base, excitation_held, inverse_held
            )
        else:
            total, kept = last_step(meta, blocks, pieces, outputs, base)
    return (kept.reshape(steps, rows, width), total.reshape(1, rows, width))


def solution(mesh):
    in_specs = (
        P(None, "rows", None),
        P("lag", "rows", None),
        P("rows", None, None),
        P(("rows", "lag"), None, None),
        P(("rows", "lag")),
        P(("rows", "lag")),
        P(("rows", "lag")),
        P(("rows", "lag"), None, None),
        P("rows", "lag"),
    )
    out_specs = (P(None, "rows", None), P("lag", "rows", None))
    return jax.shard_map(
        per_device, mesh=mesh, in_specs=in_specs, out_specs=out_specs, check_vma=False
    )
```

```python
import functools

import jax
import jax.numpy as jnp
from jax import lax
from jax.experimental import pallas as pl
from jax.experimental.pallas import tpu as pltpu
from jax.sharding import PartitionSpec as P


GROUP = 4
UNROLL = 14
GROUPS = 28
PLACES = GROUP * GROUPS
ZERO_COLUMN = 32
COUNT_WORD = PLACES + GROUPS
PIECES = 8


def accumulate(meta, blocks, pieces, base, gathered, sums):
    rows = base.shape[0]
    for place, piece in enumerate(pieces):
        gathered[pl.ds(place * rows, rows)] = piece[...]
    gathered[ZERO_COLUMN] = jnp.zeros(gathered.shape[1:], gathered.dtype)
    sums[...] = base[...]

    def several(at, carry):
        for offset in range(UNROLL):
            group = at * UNROLL + offset
            words = [meta[group * GROUP + member] for member in range(GROUP)]
            left = jnp.concatenate([blocks[word >> 6] for word in words], axis=1)
            right = jnp.concatenate([gathered[word & 63] for word in words], axis=0)
            sums[meta[PLACES + group]] += jnp.dot(left, right, preferred_element_type=jnp.float32)
        return carry

    lax.fori_loop(0, (meta[COUNT_WORD] + UNROLL - 1) // UNROLL, several, 0)


def parts(value):
    high = value.astype(jnp.bfloat16)
    return high, (value - high.astype(jnp.float32)).astype(jnp.bfloat16)


def solve(inverse, excitation, field, solved):
    for b in range(inverse.shape[0]):
        high, low = parts(inverse[b])
        right_high, right_low = parts(excitation[b].astype(jnp.float32) - field[b])
        solved[b] = jnp.dot(
            jnp.concatenate([high, high, low], axis=1),
            jnp.concatenate([right_high, right_low, right_high], axis=0),
            preferred_element_type=jnp.float32,
        ).astype(solved.dtype)


def words_kernel(tables, *refs):
    kept, held_refs, (words, tally, arrivals) = refs[:3], refs[4:7], (refs[3],) + refs[7:]
    moves = [
        pltpu.make_async_copy(source, target, arrivals.at[at])
        for at, (source, target) in enumerate(zip(kept, held_refs))
    ]
    for copy in moves:
        copy.start()
    slots = (tables.shape[0] - 2 * PIECES - 2) // 3
    live = tables[3 * slots + 2 * PIECES]
    rows = tally.shape[0]
    for b in range(rows):
        tally[b] = 0

    def clear(at, carry):
        words[at] = jnp.where(at < PLACES, ZERO_COLUMN, 0)
        return carry

    lax.fori_loop(0, COUNT_WORD + 1, clear, 0, unroll=3)

    def count_row(slot, carry):
        tally[tables[slot]] += 1
        return carry

    lax.fori_loop(0, live, count_row, 0)
    first = 0
    for b in range(rows):
        groups = (tally[b] + GROUP - 1) // GROUP

        def name_row(group, carry, b=b):
            words[PLACES + group] = b
            return carry

        tally[b] = first * GROUP
        lax.fori_loop(first, first + groups, name_row, 0)
        first = first + groups
    words[COUNT_WORD] = first

    def put(slot, carry):
        row = tables[slot]
        place = tally[row]
        tally[row] = place + 1
        owner = tables[slots + slot]
        apart = owner ^ tables[tables.shape[0] - 1]
        piece = (apart & 1) * (PIECES // 2) + (apart >> 1)
        local = tables[3 * slots + tables[2 * slots + slot] * PIECES + owner]
        words[place] = slot * 64 + piece * rows + local
        return carry

    lax.fori_loop(0, live, put, 0)
    for copy in moves:
        copy.wait()


def first_kernel(lag, excitation, base, inverse, solved, right, field, factors, arrivals):
    @pl.when(lag[0] == 0)
    def _():
        copies = [
            pltpu.make_async_copy(excitation.at[0], right, arrivals.at[0]),
            pltpu.make_async_copy(base, field, arrivals.at[1]),
            pltpu.make_async_copy(inverse, factors, arrivals.at[2]),
        ]
        for copy in copies:
            copy.start()
        for copy in copies:
            copy.wait()
        solve(factors, right, field, solved)

    @pl.when(lag[0] != 0)
    def _():
        solved[...] = jnp.zeros(solved.shape, solved.dtype)


def chain_kernel(t, lag, meta, blocks, *refs):
    pieces, (base, excitation, inverse, solved, gathered, sums) = refs[:PIECES], refs[PIECES:]

    @pl.when(lag[0] == 0)
    def _():
        accumulate(meta, blocks, pieces, base, gathered, sums)
        solve(inverse, excitation.at[t], sums, solved)

    @pl.when(lag[0] != 0)
    def _():
        solved[...] = jnp.zeros(solved.shape, solved.dtype)


def others_kernel(lag, meta, blocks, *refs):
    pieces, (base, total, gathered) = refs[:PIECES], refs[PIECES:]

    @pl.when(lag[0] != 0)
    def _():
        accumulate(meta, blocks, pieces, base, gathered, total)

    @pl.when(lag[0] == 0)
    def _():
        total[...] = jnp.zeros(total.shape, total.dtype)


def last_kernel(meta, blocks, *refs):
    pieces, solved, (base, total, kept, gathered, placed) = refs[:PIECES], refs[PIECES:-5], refs[-5:]
    copies = [
        pltpu.make_async_copy(each, kept.at[t], placed.at[t]) for t, each in enumerate(solved)
    ]
    for copy in copies:
        copy.start()
    accumulate(meta, blocks, pieces, base, gathered, total)
    for copy in copies:
        copy.wait()


PARAMS = pltpu.CompilerParams(vmem_limit_bytes=24 * 1024 * 1024)
SMEM = pl.BlockSpec(memory_space=pltpu.SMEM)
VMEM = pl.BlockSpec(memory_space=pltpu.VMEM)
ANY = pl.BlockSpec(memory_space=pl.ANY)
HBM = pl.BlockSpec(memory_space=pltpu.HBM)


def held(arrays):
    return [pltpu.with_memory_space_constraint(array, pltpu.VMEM) for array in arrays]


def gathering(base):
    return pltpu.VMEM((ZERO_COLUMN + 1,) + base.shape[1:], jnp.bfloat16)


def prepare(tables, kept, row_blocks):
    shapes = [jax.ShapeDtypeStruct(each.shape, each.dtype) for each in kept]
    words, *held_arrays = pl.pallas_call(
        words_kernel,
        out_shape=[jax.ShapeDtypeStruct((COUNT_WORD + 1,), jnp.int32)] + shapes,
        in_specs=[SMEM] + [HBM] * len(kept),
        compiler_params=pltpu.CompilerParams(vmem_limit_bytes=48 * 1024 * 1024),
        out_specs=[SMEM] + [VMEM] * len(kept),
        scratch_shapes=[
            pltpu.SMEM((row_blocks,), jnp.int32),
            pltpu.SemaphoreType.DMA((len(kept),)),
        ],
    )(tables, *kept)
    return words, held(held_arrays)


def first_solve(lag, excitation, base, inverse):
    return pl.pallas_call(
        first_kernel,
        out_shape=jax.ShapeDtypeStruct(base.shape, jnp.bfloat16),
        in_specs=[SMEM, HBM, HBM, HBM],
        out_specs=VMEM,
        scratch_shapes=[
            pltpu.VMEM(base.shape, jnp.bfloat16),
            pltpu.VMEM(base.shape, jnp.float32),
            pltpu.VMEM(inverse.shape, jnp.float32),
            pltpu.SemaphoreType.DMA((3,)),
        ],
    )(lag, excitation, base, inverse)


def chain_step(t, lag, meta, blocks, pieces, base, excitation, inverse):
    return pl.pallas_call(
        functools.partial(chain_kernel, t),
        out_shape=jax.ShapeDtypeStruct(base.shape, jnp.bfloat16),
        in_specs=[SMEM, SMEM, VMEM] + [VMEM] * PIECES + [VMEM] * 3,
        compiler_params=PARAMS,
        out_specs=VMEM,
        scratch_shapes=[gathering(base), pltpu.VMEM(base.shape, jnp.float32)],
    )(lag, meta, blocks, *held(pieces), base, excitation, inverse)


def others_step(lag, meta, blocks, pieces, base):
    return pl.pallas_call(
        others_kernel,
        out_shape=jax.ShapeDtypeStruct(base.shape, jnp.float32),
        in_specs=[SMEM, SMEM, VMEM] + [VMEM] * PIECES + [VMEM],
        compiler_params=PARAMS,
        out_specs=VMEM,
        scratch_shapes=[gathering(base)],
    )(lag, meta, blocks, *held(pieces), base)


def last_step(meta, blocks, pieces, solved, base):
    return pl.pallas_call(
        last_kernel,
        out_shape=(
            jax.ShapeDtypeStruct(base.shape, jnp.float32),
            jax.ShapeDtypeStruct((len(solved),) + base.shape, jnp.bfloat16),
        ),
        in_specs=[SMEM, VMEM] + [VMEM] * PIECES + [ANY] * len(solved) + [VMEM],
        compiler_params=PARAMS,
        out_specs=(VMEM, ANY),
        scratch_shapes=[gathering(base), pltpu.SemaphoreType.DMA((len(solved),))],
    )(meta, blocks, *held(pieces), *solved, base)


def over_rows(value, flip):
    count = lax.axis_size("rows")
    return lax.ppermute(value, "rows", [(r, r ^ flip) for r in range(count)])


def exchange(own):
    half = lax.axis_size("rows") // 2
    near = [own]
    for z in range(1, half):
        near.append(over_rows(own, 2 * z))
    pieces = list(near)
    for z in range(half):
        pieces.append(over_rows(near[z], 1))
    return pieces


LAG_ROUNDS = (
    [(0, 1)],
    [(0, 3), (1, 2)],
    [(x, x + 4) for x in range(4)],
    [(x, x + 12) for x in range(4)] + [(x + 4, x + 8) for x in range(4)],
)


def spread(value):
    lag = lax.axis_index("lag")
    for pairs in LAG_ROUNDS:
        arrived = lax.ppermute(value, "lag", pairs)
        takes = jnp.zeros((), jnp.bool_)
        for _, target in pairs:
            takes = takes | (lag == target)
        value = jnp.where(takes, arrived, value)
    return value


def from_behind(value):
    count = lax.axis_size("lag")
    return lax.ppermute(value, "lag", [(g + 1, g) for g in range(count - 1)])


def per_device(
    excitation, pending, inverse, interaction, slot_row, slot_owner, slot_pos, needed, block_count
):
    row_blocks, block_size, _ = inverse.shape
    steps, rows, width = excitation.shape
    excitation_blocks = excitation.reshape(steps, row_blocks, block_size, width)
    lag = jnp.full((1,), lax.axis_index("lag"), jnp.int32)
    row_owner = jnp.full((1,), lax.axis_index("rows"), jnp.int32)
    total = pending[0].reshape(row_blocks, block_size, width)
    solved = first_solve(lag, excitation_blocks, total, inverse)
    tables = (slot_row, slot_owner, slot_pos, needed.transpose(0, 2, 1), block_count, row_owner)
    tables = jnp.concatenate([table.reshape(-1) for table in tables])
    meta, (blocks, excitation_held, inverse_held) = prepare(
        tables, (interaction, excitation_blocks, inverse), row_blocks
    )
    outputs = []
    for t in range(steps):
        solved = spread(solved)
        outputs.append(solved)
        if t > 0:
            total = others_step(lag, meta, blocks, pieces, base)
        base = from_behind(total)
        pieces = exchange(solved)
        if t + 1 < steps:
            solved = chain_step(
                t + 1, lag, meta, blocks, pieces, base, excitation_held, inverse_held
            )
        else:
            total, kept = last_step(meta, blocks, pieces, outputs, base)
    return (kept.reshape(steps, rows, width), total.reshape(1, rows, width))


def solution(mesh):
    in_specs = (
        P(None, "rows", None),
        P("lag", "rows", None),
        P("rows", None, None),
        P(("rows", "lag"), None, None),
        P(("rows", "lag")),
        P(("rows", "lag")),
        P(("rows", "lag")),
        P(("rows", "lag"), None, None),
        P("rows", "lag"),
    )
    out_specs = (P(None, "rows", None), P("lag", "rows", None))
    return jax.shard_map(
        per_device, mesh=mesh, in_specs=in_specs, out_specs=out_specs, check_vma=False
    )
```
